32 devices in a mesh: groups: 2 (over x), rows: 16 (over z, y, core).
Axes of the slice: x: 2, y: 2, z: 4, core: 2. Of those that a mesh axis runs over, the one named last changes fastest.
Arguments:
- features: float32 [448, 14, 192], P(('groups', 'rows')), parts along dimension 0, may hold values from -6 to 6
- fine_gain_one: float32 [192], replicated, may hold values from 0.1 to 1.9
- fine_project_in: float32 [192, 576], replicated, may hold values from -30 to 30
- fine_project_out: float32 [192, 192], replicated, may hold values from -0.4375 to 0.4375
- fine_gain_two: float32 [192], replicated, may hold values from 0.1 to 1.9
- fine_expand: float32 [192, 768], replicated, may hold values from -0.4375 to 0.4375
- fine_contract: float32 [768, 192], replicated, may hold values from -0.21875 to 0.21875
- merge_gain: float32 [768], replicated, may hold values from 0.1 to 1.9
- merge_weight: float32 [768, 384], replicated, may hold values from -0.21875 to 0.21875
- coarse_gain: float32 [384], replicated, may hold values from 0.1 to 1.9
- coarse_project_in: float32 [384, 1152], replicated, may hold values from -30 to 30
- coarse_project_out: float32 [384, 384], replicated, may hold values from -0.3125 to 0.3125
- cotangent: float32 [224, 7, 384], P(('groups', 'rows')), parts along dimension 0, may hold values from -6 to 6
Outputs:
- coarse_out: float32 [224, 7, 384], P(('groups', 'rows')), parts along dimension 0
- gradient_features: float32 [448, 14, 192], P(('groups', 'rows')), parts along dimension 0
- gradient_fine_gain_one: float32 [384], P('groups'), parts along dimension 0
- gradient_fine_project_in: float32 [384, 576], P('groups'), parts along dimension 0
- gradient_fine_project_out: float32 [384, 192], P('groups'), parts along dimension 0
- gradient_fine_gain_two: float32 [384], P('groups'), parts along dimension 0
- gradient_fine_expand: float32 [384, 768], P('groups'), parts along dimension 0
- gradient_fine_contract: float32 [1536, 192], P('groups'), parts along dimension 0
- gradient_merge_gain: float32 [1536], P('groups'), parts along dimension 0
- gradient_merge_weight: float32 [1536, 384], P('groups'), parts along dimension 0
- gradient_coarse_gain: float32 [768], P('groups'), parts along dimension 0
- gradient_coarse_project_in: float32 [768, 1152], P('groups'), parts along dimension 0
- gradient_coarse_project_out: float32 [768, 384], P('groups'), parts along dimension 0
The draws below stay inside these ranges and needn't reach their ends.
There are 2 independent parts, one for each index of `groups`. The reference program is written for one: setup_inputs(seed, part) draws one part's arguments, and reference() takes and returns one part's arrays. A program takes and returns all parts, laid end to end along the dimension named above; an argument that names none is the same for every part. Nothing has to cross between parts.
All inputs are finite; a program needn't handle non-finite values.
Results may differ from the reference program's by a relative error of at most 0.0004.
Values sent between devices are 32-bit elements; how exact they have to be, the bound alone decides.
A program may use at most 128 MiB of HBM per device.

```python
import jax
import jax.numpy as jnp
from jax import lax

C_FINE = 192
HEAD_DIM = 32
FEED_UNITS = 768
W_COLS = 14
C_COARSE = 384
HT = 224


def draw_projection(key, channels):
    base = jax.random.truncated_normal(key, -4.0, 4.0, (channels, 3 * channels), jnp.float32) * channels ** (-0.5)
    return base


def draw_fine_project_in(key, part):
    return draw_projection(jax.random.fold_in(key, 11), C_FINE)


def draw_coarse_project_in(key, part):
    return draw_projection(jax.random.fold_in(key, 23), C_COARSE)


def shard_levels(own_key, dims, split, least, largest):
    def one(position, parts):
        draws = jax.random.uniform(jax.random.fold_in(jax.random.fold_in(own_key, 6), position), (parts,), jnp.float32, least / len(split), largest / len(split))
        return jnp.repeat(jnp.exp(draws), dims[position] // parts).reshape((-1,) + (1,) * (len(dims) - position - 1))

    factor_of = one(*split[0])
    for cut in split[1:]:
        factor_of = factor_of * one(*cut)
    return factor_of


def scatter_about(own_key, dims, scale, most, shards=(), held_as=jnp.bfloat16):
    loudness = shard_levels(own_key, dims, shards, -0.22, 0.18) if shards else 1.0
    values = jax.random.normal(own_key, dims, jnp.float32) * scale * loudness
    return jnp.minimum(jnp.maximum(values, -most), most).astype(held_as)


def setup_inputs(seed: int = 0, part: int = 0) -> dict:
    splits = jax.random.split(jax.random.key(seed), 14)
    part_keys = jax.random.split(jax.random.fold_in(splits[13], part), 14)
    return {
        "features": scatter_about(part_keys[0], (HT, W_COLS, C_FINE), 1.0, 6.0, ((0, 16),), jnp.float32),
        "fine_gain_one": jnp.clip(1.0 + 0.18 * jax.random.normal(splits[1], (C_FINE,), jnp.float32), 0.1, 1.9),
        "fine_project_in": draw_fine_project_in(jax.random.fold_in(splits[13], 71), part),
        "fine_project_out": scatter_about(splits[3], (C_FINE, C_FINE), C_FINE ** -0.5, 0.4375, (), jnp.float32),
        "fine_gain_two": jnp.clip(1.0 + 0.18 * jax.random.normal(splits[4], (C_FINE,), jnp.float32), 0.1, 1.9),
        "fine_expand": scatter_about(splits[5], (C_FINE, FEED_UNITS), C_FINE ** -0.5, 0.4375, (), jnp.float32),
        "fine_contract": scatter_about(splits[6], (FEED_UNITS, C_FINE), FEED_UNITS ** -0.5, 0.21875, (), jnp.float32),
        "merge_gain": jnp.clip(1.0 + 0.18 * jax.random.normal(splits[7], (4 * C_FINE,), jnp.float32), 0.1, 1.9),
        "merge_weight": scatter_about(splits[8], (4 * C_FINE, C_COARSE), (4 * C_FINE) ** -0.5, 0.21875, (), jnp.float32),
        "coarse_gain": jnp.clip(1.0 + 0.18 * jax.random.normal(splits[9], (C_COARSE,), jnp.float32), 0.1, 1.9),
        "coarse_project_in": draw_coarse_project_in(jax.random.fold_in(splits[13], 71), part),
        "coarse_project_out": scatter_about(splits[11], (C_COARSE, C_COARSE), C_COARSE ** -0.5, 0.3125, (), jnp.float32),
        "cotangent": scatter_about(part_keys[12], (HT // 2, W_COLS // 2, C_COARSE), 1.0, 6.0, ((0, 16),), jnp.float32),
    }


EPSILON = 1e-05
PRECISE = lax.Precision.HIGHEST

def layer_norm(values_in, gain_vec):
    average = lax.optimization_barrier(jnp.mean(values_in, axis=-1, keepdims=True))
    centered = values_in - average
    variance = lax.optimization_barrier(jnp.mean(centered * centered, axis=-1, keepdims=True))
    return centered * lax.rsqrt(variance + EPSILON) * gain_vec

def window_attention(window_slab, labels, weight_in, weight_out, head_size):
    slab_rows, slab_cols, channels = window_slab.shape
    head_count = channels // head_size
    win_rows = slab_rows // 7
    win_cols = slab_cols // 7
    count = win_rows * win_cols
    windows = window_slab.reshape(win_rows, 7, win_cols, 7, channels).transpose(0, 2, 1, 3, 4).reshape(count, 49, channels)
    label_win = labels.reshape(win_rows, 7, win_cols, 7).transpose(0, 2, 1, 3).reshape(count, 49)
    projected = jnp.einsum('nqc,cf->nqf', windows, weight_in, precision=PRECISE)
    projected = projected.reshape(count, 49, 3, head_count, head_size)
    queries = projected[:, :, 0]
    key_rows = projected[:, :, 1]
    value_rows = projected[:, :, 2]
    scores = jnp.einsum('nqhd,nkhd->nhqk', queries, key_rows, precision=PRECISE) * head_size ** (-0.5)
    allowed = label_win[:, None, :, None] == label_win[:, None, None, :]
    scores = jnp.where(allowed, scores, -1e+30)
    row_max = lax.optimization_barrier(jnp.max(scores, axis=-1, keepdims=True))
    weights = jnp.exp(scores - row_max)
    weights = weights / lax.optimization_barrier(jnp.sum(weights, axis=-1, keepdims=True))
    context = jnp.einsum('nhqk,nkhd->nqhd', weights, value_rows, precision=PRECISE).reshape(count, 49, channels)
    result = jnp.einsum('nqc,cf->nqf', context, weight_out, precision=PRECISE)
    return result.reshape(win_rows, win_cols, 7, 7, channels).transpose(0, 2, 1, 3, 4).reshape(slab_rows, slab_cols, channels)

def shifted_block(residual, gain_vec, project_in, project_out):
    all_rows, breadth = (residual.shape[0], residual.shape[1])
    normed = layer_norm(residual, gain_vec)
    rolled = jnp.roll(normed, (-3, -3), (0, 1))
    row_flag = (jnp.arange(all_rows) >= all_rows - 3).astype(jnp.int32)
    col_flag = (jnp.arange(breadth) >= breadth - 3).astype(jnp.int32)
    labels = row_flag[:, None] * 2 + col_flag[None, :]
    attended = window_attention(rolled, labels, project_in, project_out, HEAD_DIM)
    return residual + jnp.roll(attended, (3, 3), (0, 1))

def feed_forward(residual, gain_vec, expand, contract):
    normed = layer_norm(residual, gain_vec)
    inner = jax.nn.gelu(jnp.dot(normed, expand, precision=PRECISE), approximate=False)
    return residual + jnp.dot(inner, contract, precision=PRECISE)

def patch_merge(grid, gain_vec, weight):
    height, breadth, channels = grid.shape
    blocks = grid.reshape(height // 2, 2, breadth // 2, 2, channels).transpose(0, 2, 3, 1, 4)
    blocks = blocks.reshape(height // 2, breadth // 2, 4 * channels)
    return jnp.dot(layer_norm(blocks, gain_vec), weight, precision=PRECISE)

def forward(features, fine_gain_one, fine_project_in, fine_project_out, fine_gain_two, fine_expand, fine_contract, merge_gain, merge_weight, coarse_gain, coarse_project_in, coarse_project_out):
    fine_mid = shifted_block(features, fine_gain_one, fine_project_in, fine_project_out)
    fine_done = feed_forward(fine_mid, fine_gain_two, fine_expand, fine_contract)
    merged = patch_merge(fine_done, merge_gain, merge_weight)
    return shifted_block(merged, coarse_gain, coarse_project_in, coarse_project_out)

def reference(features, fine_gain_one, fine_project_in, fine_project_out, fine_gain_two, fine_expand, fine_contract, merge_gain, merge_weight, coarse_gain, coarse_project_in, coarse_project_out, cotangent):
    coarse_out, pullback = jax.vjp(forward, features, fine_gain_one, fine_project_in, fine_project_out, fine_gain_two, fine_expand, fine_contract, merge_gain, merge_weight, coarse_gain, coarse_project_in, coarse_project_out)
    grads = pullback(cotangent)
    grad_scale = 1.0 / jnp.sqrt(jnp.float32(coarse_out.shape[0] * coarse_out.shape[1]))
    scaled = [grads[index] * grad_scale for index in range(1, 12)]
    return (coarse_out, grads[0], scaled[0], scaled[1], scaled[2], scaled[3], scaled[4], scaled[5], scaled[6], scaled[7], scaled[8], scaled[9], scaled[10])
```

```python
import functools

import jax
import jax.numpy as jnp
from jax import lax
from jax.experimental import pallas as pl
from jax.experimental.pallas import tpu as pltpu
from jax.sharding import PartitionSpec as P

HEAD_DIM = 32
WIN = 7
PAD = 8
TOK = PAD * PAD
SHIFT = 3
EPSILON = 1e-05
MESH = pl.DeviceIdType.MESH
F32 = jnp.float32
BF16 = jnp.bfloat16
NN = (((1,), (0,)), ((), ()))
NT = (((1,), (1,)), ((), ()))
TN = (((0,), (0,)), ((), ()))


def halves(a):
    hi = a.astype(BF16)
    return hi, (a - hi.astype(F32)).astype(BF16)


def mm(a, b, dims=NN):
    a = a if isinstance(a, tuple) else halves(a)
    b = b if isinstance(b, tuple) else halves(b)
    dot = functools.partial(lax.dot_general, dimension_numbers=dims, preferred_element_type=F32)
    return dot(a[0], b[0]) + (dot(a[0], b[1]) + dot(a[1], b[0]))


def runs(first, count, breadth):
    head = min(count, breadth - first % breadth)
    pieces = [(0, first % breadth, head)]
    return pieces + ([(head, 0, count - head)] if head < count else [])


def take_windows(dst, first_rows, slab_ref, skip, last_rows, win_cols):
    breadth = slab_ref.shape[1]
    sources = [(r, i) for r in (first_rows,) if r is not None for i in range(r.shape[0])]
    sources += [(slab_ref, i) for i in range(skip, slab_ref.shape[0])]
    sources += [(r, i) for r in (last_rows,) if r is not None for i in range(r.shape[0])]
    dst[...] = jnp.zeros_like(dst)
    for w in range(dst.shape[0]):
        row, col = divmod(w, win_cols)
        for i in range(WIN):
            ref, at = sources[row * WIN + i]
            for place, start, size in runs(col * WIN + SHIFT, WIN, breadth):
                dst[w, i, place : place + size, :] = ref[at, start : start + size, :]


def put_windows(dst, src, win_cols):
    breadth = dst.shape[1]
    for w in range(src.shape[0]):
        row, col = divmod(w, win_cols)
        for place, start, size in runs(col * WIN + SHIFT, WIN, breadth):
            dst[row * WIN : (row + 1) * WIN, start : start + size, :] = src[
                w, :WIN, place : place + size, :
            ]


def norm(v):
    centered = v - jnp.mean(v, axis=-1, keepdims=True)
    scale = lax.rsqrt(jnp.mean(centered * centered, axis=-1, keepdims=True) + EPSILON)
    return centered * scale, scale


def norm_back(dn, n, scale):
    return scale * (
        dn - jnp.mean(dn, axis=-1, keepdims=True) - n * jnp.mean(dn * n, axis=-1, keepdims=True)
    )


def spread(a, heads):
    lane = lax.broadcasted_iota(jnp.int32, a.shape, 1) // HEAD_DIM
    return jnp.concatenate([jnp.where(lane == h, a, 0.0) for h in range(heads)], axis=0)


def gather_heads(a, heads):
    rows = a.shape[0] // heads
    lane = lax.broadcasted_iota(jnp.int32, (rows, a.shape[1]), 1) // HEAD_DIM
    total = jnp.where(lane == 0, a[:rows], 0.0)
    for h in range(1, heads):
        total = jnp.where(lane == h, a[h * rows : (h + 1) * rows], total)
    return total


def allowed(last_row, last_col):
    def label(axis):
        t = lax.broadcasted_iota(jnp.int32, (TOK, TOK), axis)
        r, c = t // PAD, t % PAD
        lab = jnp.where(r >= WIN - SHIFT, last_row * 2, 0) + jnp.where(
            c >= WIN - SHIFT, last_col, 0
        )
        return lab, (r < WIN) & (c < WIN)

    lq, _ = label(0)
    lk, real = label(1)
    return (lq == lk) & real


def attend(q, k, v, mask, heads):
    s = mm(spread(q, heads), k, NT) * HEAD_DIM**-0.5
    s = jnp.where(jnp.concatenate([mask] * heads, axis=0), s, -1e30)
    w = jnp.exp(s - jnp.max(s, axis=-1, keepdims=True))
    w = w / jnp.sum(w, axis=-1, keepdims=True)
    return w, gather_heads(mm(w, v), heads)


def attend_back(dctx, q, k, v, w, heads):
    dc = halves(spread(dctx, heads))
    dw = mm(dc, v, NT)
    dv = mm(w, dc, TN)
    ds = w * (dw - jnp.sum(dw * w, axis=-1, keepdims=True)) * HEAD_DIM**-0.5
    ds = halves(ds)
    dq = gather_heads(mm(ds, k), heads)
    dk = mm(ds, spread(q, heads), TN)
    return dq, dk, dv


def fine_forward(
    win_cols, last_ref, f_ref, halo_ref, g_ref, win_ref, wout_ref, mid_ref, head_ref, x_ref, qkv_ref, w_ref, ctx_ref, cells
):
    channels = x_ref.shape[1]
    heads = channels // HEAD_DIM
    windows = cells.shape[0]
    take_windows(cells, None, f_ref, SHIFT, halo_ref, win_cols)
    x = cells[...].reshape(windows * TOK, channels)
    x_ref[...] = x
    n, _ = norm(x)
    u = halves(n * g_ref[...])
    parts = []
    for part in range(3):
        got = mm(u, win_ref[:, part * channels : (part + 1) * channels])
        qkv_ref[part] = got
        parts.append(got)
    for i in range(windows):
        row, col = divmod(i, win_cols)
        bottom = last_ref[0] if row == windows // win_cols - 1 else 0
        mask = allowed(bottom, int(col == win_cols - 1))
        at = slice(i * TOK, (i + 1) * TOK)
        w, ctx = attend(parts[0][at], parts[1][at], parts[2][at], mask, heads)
        w_ref[i] = w
        ctx_ref[at, :] = ctx
    mid = x + mm(ctx_ref[...], wout_ref[...])
    cells[...] = mid.reshape(cells.shape)
    put_windows(mid_ref, cells, win_cols)
    head_ref[...] = mid_ref[:SHIFT]


def fine_backward(
    grad_scale, first, win_cols, d_ref, prefix_ref, x_ref, g_ref, win_ref, wout_ref, qkv_ref, w_ref, ctx_ref, _, dx_ref, tail_ref, pack_ref, own, cells, sem
):
    channels = x_ref.shape[1]
    heads = channels // HEAD_DIM
    windows = x_ref.shape[0] // TOK
    take_windows(cells, prefix_ref, d_ref, 0, None, win_cols)
    d = cells[...].reshape(x_ref.shape)
    n, scale = norm(x_ref[...])
    g = g_ref[...]
    u = halves(n * g)
    dh = halves(d)
    dctx = mm(dh, wout_ref[...], NT)
    dwout = mm(ctx_ref[...], dh, TN)
    grads = ([], [], [])
    for i in range(windows):
        at = slice(i * TOK, (i + 1) * TOK)
        got = attend_back(dctx[at], qkv_ref[0, at], qkv_ref[1, at], qkv_ref[2, at], w_ref[i], heads)
        for group, part in zip(grads, got):
            group.append(part)
    du = 0.0
    weight = []
    for part in range(3):
        dp = halves(jnp.concatenate(grads[part], axis=0))
        du += mm(dp, win_ref[:, part * channels : (part + 1) * channels], NT)
        weight.append(mm(u, dp, TN) * grad_scale)
    own[:channels, :] = jnp.concatenate(weight[:2], axis=1)
    own[channels : 2 * channels, :] = jnp.concatenate([weight[2], dwout * grad_scale], axis=1)
    own[2 * channels :, :] = jnp.zeros_like(own[2 * channels :, :])
    own[2 * channels : 2 * channels + 1, :channels] = (
        jnp.sum(du * n, axis=0, keepdims=True) * grad_scale
    )
    copy = pltpu.make_async_copy(own, pack_ref.at[pl.ds(first, own.shape[0])], sem)
    copy.start()
    cells[...] = (d + norm_back(du * g, n, scale)).reshape(cells.shape)
    put_windows(dx_ref, cells, win_cols)
    tail_ref[...] = dx_ref[dx_ref.shape[0] - SHIFT :]
    copy.wait()


def middle(
    grad_scale,
    spot,
    last_ref,
    mid_ref,
    halo_ref,
    cotangent_ref,
    cot_halo_ref,
    g2_ref,
    we_ref,
    wc_ref,
    gm_ref,
    wm_ref,
    gc_ref,
    win_ref,
    wout_ref,
    out_ref,
    out_tail_ref,
    dmid_ref,
    dmid_tail_ref,
    pack_ref,
    h_ref,
    act_ref,
    quads,
    cells,
):
    height, breadth, cf = mid_ref.shape
    cc = cotangent_ref.shape[2]
    heads = cc // HEAD_DIM
    quads[...] = jnp.zeros_like(quads)
    for k in range(4):
        dj, di = divmod(k, 2)
        for i in range(WIN):
            r = SHIFT + 2 * i + di
            ref, r = (mid_ref, r) if r < height else (halo_ref, r - height)
            for j in range(WIN):
                at = (2 * (SHIFT + j) + dj) % breadth
                quads[k, i, j : j + 1, :] = ref[r, at : at + 1, :]
    x = quads[...].reshape(4 * TOK, cf)
    n2, r2 = norm(x)
    g2 = g2_ref[...]
    u2 = halves(n2 * g2)
    h = mm(u2, we_ref[...])
    h_ref[...] = h
    act = h * (0.5 * (1.0 + lax.erf(h * 0.5**0.5)))
    act_ref[...] = act
    y = x + mm(act, wc_ref[...], NT)
    ys = [y[k * TOK : (k + 1) * TOK] for k in range(4)]
    wide = 1.0 / (4 * cf)
    mean = sum(jnp.sum(v, axis=-1, keepdims=True) for v in ys) * wide
    ys = [v - mean for v in ys]
    rm = lax.rsqrt(sum(jnp.sum(v * v, axis=-1, keepdims=True) for v in ys) * wide + EPSILON)
    nm = [v * rm for v in ys]
    gm = [gm_ref[k : k + 1, :] for k in range(4)]
    um = [halves(nm[k] * gm[k]) for k in range(4)]
    merged = sum(mm(um[k], wm_ref[k * cf : (k + 1) * cf, :]) for k in range(4))
    nc, rc = norm(merged)
    gc = gc_ref[...]
    uc = halves(nc * gc)
    q, k_, v_ = (mm(uc, win_ref[:, p * cc : (p + 1) * cc]) for p in range(3))
    w, ctx = attend(q, k_, v_, allowed(last_ref[0], 1), heads)
    cells[0] = (merged + mm(ctx, wout_ref[...])).reshape(PAD, PAD, cc)
    put_windows(out_ref, cells, 1)
    out_tail_ref[...] = out_ref[WIN - SHIFT :]
    take_windows(cells, None, cotangent_ref, SHIFT, cot_halo_ref, 1)
    cot = cells[0].reshape(TOK, cc)
    ch = halves(cot)
    pack_ref[spot["coarse_out"] : spot["coarse_out"] + cc, :] = mm(ctx, ch, TN) * grad_scale
    dctx = mm(ch, wout_ref[...], NT)
    got = attend_back(dctx, q, k_, v_, w, heads)
    du = 0.0
    for p in range(3):
        dp = halves(got[p])
        top = spot["coarse_in"] + p * cc
        pack_ref[top : top + cc, :] = mm(uc, dp, TN) * grad_scale
        du += mm(dp, win_ref[:, p * cc : (p + 1) * cc], NT)
    gains = spot["gains"]
    pack_ref[gains:, :] = jnp.zeros_like(pack_ref[gains:, :])
    pack_ref[gains + 3 : gains + 4, :] = jnp.sum(du * nc, axis=0, keepdims=True) * grad_scale
    dm = cot + norm_back(du * gc, nc, rc)
    mh = halves(dm)
    dn = []
    for k in range(4):
        top = spot["merge"] + k * cf
        pack_ref[top : top + cf, :] = mm(um[k], mh, TN) * grad_scale
        dk = mm(mh, wm_ref[k * cf : (k + 1) * cf, :], NT)
        row = gains + 1 + k // 2
        pack_ref[row : row + 1, (k % 2) * cf : (k % 2 + 1) * cf] = jnp.sum(dk * nm[k], axis=0, keepdims=True) * grad_scale
        dn.append(dk * gm[k])
    m1 = sum(jnp.sum(v, axis=-1, keepdims=True) for v in dn) * wide
    m2 = sum(jnp.sum(dn[k] * nm[k], axis=-1, keepdims=True) for k in range(4)) * wide
    dy = jnp.concatenate([rm * (dn[k] - m1 - nm[k] * m2) for k in range(4)], axis=0)
    yh = halves(dy)
    dwc = mm(yh, act_ref[...], TN) * grad_scale
    top = spot["contract"]
    for p in range(dwc.shape[1] // cc):
        pack_ref[top + p * cf : top + (p + 1) * cf, :] = dwc[:, p * cc : (p + 1) * cc]
    h = h_ref[...]
    slope = 0.5 * (1.0 + lax.erf(h * 0.5**0.5)) + h * (jnp.exp(-0.5 * h * h) * 0.3989422804014327)
    dh = halves(mm(yh, wc_ref[...]) * slope)
    dwe = mm(u2, dh, TN) * grad_scale
    top = spot["expand"]
    for p in range(dwe.shape[1] // cc):
        pack_ref[top + p * cf : top + (p + 1) * cf, :] = dwe[:, p * cc : (p + 1) * cc]
    du2 = mm(dh, we_ref[...], NT)
    pack_ref[gains : gains + 1, :cf] = jnp.sum(du2 * n2, axis=0, keepdims=True) * grad_scale
    quads[...] = (dy + norm_back(du2 * g2, n2, r2)).reshape(quads.shape)
    for k in range(4):
        dj, di = divmod(k, 2)
        for i in range(WIN):
            for j in range(WIN):
                at = (2 * (SHIFT + j) + dj) % breadth
                dmid_ref[2 * i + di, at : at + 1, :] = quads[k, i, j : j + 1, :]
    dmid_tail_ref[...] = dmid_ref[height - SHIFT :]


STREAMS = 2


def ring_sum(
    chips, seg, g_ref, out_ref, pair_buf, acc, ring_buf, pair_send, pair_recv, rs_send, rs_recv, ag_send, ag_recv, back_send, back_recv
):
    me = lax.axis_index("rows")
    core, chip = me % 2, me // 2
    column, line = chip % 2, chip // 2
    at = jnp.where(column == 0, line, chips - 1 - line)
    step = 1 - 2 * core
    sub = seg // STREAMS

    def device(q):
        q = (q + chips) % chips
        return jnp.where(q < chips // 2, q * 2, (chips - 1 - q) * 2 + 1) * 2 + core

    ahead, behind, mate = device(at + step), device(at - step), me + 1 - 2 * core
    barrier = pltpu.get_barrier_semaphore()
    for other in (ahead, behind, mate):
        pl.semaphore_signal(barrier, inc=1, device_id={"rows": other}, device_id_type=MESH)
    pl.semaphore_wait(barrier, 3)

    def slot(chunk, a):
        chunk = (chunk + 2 * chips) % chips
        return pl.ds(pl.multiple_of(chunk * seg + a * sub, 8), sub)

    def rows(half, chunk, a):
        chunk = (chunk + 2 * chips) % chips
        return pl.ds(pl.multiple_of((half * chips + chunk) * seg + a * sub, 8), sub)

    def remote(src, dst, send, recv, target):
        return pltpu.make_async_remote_copy(
            src_ref=src,
            dst_ref=dst,
            send_sem=send,
            recv_sem=recv,
            device_id={"rows": target},
            device_id_type=MESH,
        )

    def pair_copy(s, a):
        chunk = at + step * s
        return remote(
            g_ref.at[rows(1 - core, chunk, a)],
            pair_buf.at[slot(chunk, a)],
            pair_send.at[s, a],
            pair_recv.at[s, a],
            mate,
        )

    def pair_arrival(s, a):
        chunk = at - step * s
        return remote(
            g_ref.at[rows(1 - core, chunk, a)],
            pair_buf.at[slot(chunk, a)],
            pair_send.at[s, a],
            pair_recv.at[s, a],
            mate,
        )

    def rs_copy(s, a):
        return remote(
            acc.at[slot(at - step * s, a)],
            ring_buf.at[s, pl.ds(a * sub, sub)],
            rs_send.at[s, a],
            rs_recv.at[s, a],
            ahead,
        )

    def ag_copy(s, a):
        where = rows(core, at + step - step * s, a)
        return remote(out_ref.at[where], out_ref.at[where], ag_send.at[s, a], ag_recv.at[s, a], ahead)

    def ag_arrival(s, a):
        where = rows(core, at - step * s, a)
        return remote(out_ref.at[where], out_ref.at[where], ag_send.at[s, a], ag_recv.at[s, a], ahead)

    def back_copy(s, a):
        where = rows(core, at + step - step * s, a)
        return remote(out_ref.at[where], out_ref.at[where], back_send.at[s, a], back_recv.at[s, a], mate)

    def back_arrival(s, a):
        where = rows(1 - core, at - step + step * s, a)
        return remote(out_ref.at[where], out_ref.at[where], back_send.at[s, a], back_recv.at[s, a], mate)

    streams = range(STREAMS)
    for s in range(chips):
        for a in streams:
            pair_copy(s, a).start()
    for s in range(chips):
        for a in streams:
            chunk = at - step * s
            pair_arrival(s, a).wait_recv()
            total = g_ref[rows(core, chunk, a), :] + pair_buf[slot(chunk, a), :]
            if s > 0:
                rs_copy(s - 1, a).wait_recv()
                total = total + ring_buf[s - 1, a * sub : (a + 1) * sub, :]
            if s < chips - 1:
                acc[slot(chunk, a), :] = total
                rs_copy(s, a).start()
            else:
                out_ref[rows(core, chunk, a), :] = total
                ag_copy(0, a).start()
                back_copy(0, a).start()
    for s in range(chips - 1):
        for a in streams:
            ag_arrival(s, a).wait_recv()
            if s < chips - 2:
                ag_copy(s + 1, a).start()
            back_copy(s + 1, a).start()
    for s in range(chips):
        for a in streams:
            pair_copy(s, a).wait_send()
            back_copy(s, a).wait_send()
            back_arrival(s, a).wait_recv()
            if s < chips - 1:
                rs_copy(s, a).wait_send()
                ag_copy(s, a).wait_send()


def all_sum(packed, devices):
    chips = devices // 2
    rows, lanes = packed.shape
    seg = rows // devices
    vmem = pl.BlockSpec(memory_space=pltpu.VMEM)
    sems = [pltpu.SemaphoreType.DMA((chips, STREAMS)) for _ in range(8)]
    return pl.pallas_call(
        functools.partial(ring_sum, chips, seg),
        out_shape=jax.ShapeDtypeStruct(packed.shape, F32),
        in_specs=[vmem],
        out_specs=vmem,
        scratch_shapes=[
            pltpu.VMEM((chips * seg, lanes), F32),
            pltpu.VMEM((chips * seg, lanes), F32),
            pltpu.VMEM((chips - 1, seg, lanes), F32),
            *sems,
        ],
        compiler_params=pltpu.CompilerParams(
            collective_id=0, has_side_effects=True, vmem_limit_bytes=28 * 2**20
        ),
        name="ring_sum",
    )(packed)


def unpack(
    spot, cf, cc, sum_ref, out_ref, out_top, dx_ref, dx_top, *rest
):
    (coarse_out, grad_features, g1, fine_in, fine_out, g2, expand, contract, gm, merge, gc, coarse_in, coarse_proj) = rest[:13]
    sems = rest[13]
    moves = [
        (out_top, coarse_out.at[pl.ds(0, SHIFT)]),
        (out_ref.at[pl.ds(0, out_ref.shape[0] - SHIFT)], coarse_out.at[pl.ds(SHIFT, out_ref.shape[0] - SHIFT)]),
        (dx_top, grad_features.at[pl.ds(0, SHIFT)]),
        (dx_ref.at[pl.ds(0, dx_ref.shape[0] - SHIFT)], grad_features.at[pl.ds(SHIFT, dx_ref.shape[0] - SHIFT)]),
        (sum_ref.at[pl.ds(spot["merge"], 4 * cf)], merge),
        (sum_ref.at[pl.ds(spot["coarse_out"], cc)], coarse_proj),
    ]
    for name, into in (("coarse_in", coarse_in), ("expand", expand), ("contract", contract)):
        size = into.shape[0]
        for p in range(into.shape[1] // cc):
            moves.append((sum_ref.at[pl.ds(spot[name] + p * size, size)], into.at[:, pl.ds(p * cc, cc)]))
    copies = [pltpu.make_async_copy(src, dst, sems.at[i]) for i, (src, dst) in enumerate(moves)]
    for copy in copies:
        copy.start()
    top = spot["fine"]
    fine_in[:, :cc] = sum_ref[top : top + cf, :]
    fine_in[:, cc:] = sum_ref[top + cf : top + 2 * cf, :cf]
    fine_out[...] = sum_ref[top + cf : top + 2 * cf, cf:]
    g1[...] = sum_ref[top + 2 * cf : top + 2 * cf + 1, :cf]
    gains = spot["gains"]
    g2[...] = sum_ref[gains : gains + 1, :cf]
    gm[:, :cc] = sum_ref[gains + 1 : gains + 2, :]
    gm[:, cc:] = sum_ref[gains + 2 : gains + 3, :]
    gc[...] = sum_ref[gains + 3 : gains + 4, :]
    for copy in copies:
        copy.wait()


def shards(
    features,
    fine_gain_one,
    fine_project_in,
    fine_project_out,
    fine_gain_two,
    fine_expand,
    fine_contract,
    merge_gain,
    merge_weight,
    coarse_gain,
    coarse_project_in,
    coarse_project_out,
    cotangent,
):
    devices = lax.axis_size("rows")
    height, breadth, cf = features.shape
    low, narrow, cc = cotangent.shape
    units = fine_expand.shape[1]
    assert low == narrow == WIN and cc == 2 * cf and units % cc == 0
    grad_scale = 1.0 / (devices * low * narrow) ** 0.5
    win_rows, win_cols = height // WIN, breadth // WIN
    count = win_rows * win_cols
    heads = cf // HEAD_DIM
    tokens = count * TOK
    last = (lax.axis_index("rows") == devices - 1).astype(jnp.int32).reshape(1)
    vmem = pl.BlockSpec(memory_space=pltpu.VMEM)
    smem = pl.BlockSpec(memory_space=pltpu.SMEM)
    anywhere = pl.BlockSpec(memory_space=pl.ANY)

    def shape(*dims):
        return jax.ShapeDtypeStruct(dims, F32)

    def limit(mib):
        return pltpu.CompilerParams(vmem_limit_bytes=mib * 2**20)

    def shift(block, distance):
        route = [((i - distance) % devices, i) for i in range(devices)]
        return lax.ppermute(block, "rows", route)

    features_below = shift(features[:SHIFT], -1)
    cotangent_below = shift(cotangent[:SHIFT], -1)
    g1 = fine_gain_one.reshape(1, cf)
    mid, mid_head, x1, qkv, weights, ctx = pl.pallas_call(
        functools.partial(fine_forward, win_cols),
        out_shape=(
            shape(height, breadth, cf),
            shape(SHIFT, breadth, cf),
            shape(tokens, cf),
            shape(3, tokens, cf),
            shape(count, heads * TOK, TOK),
            shape(tokens, cf),
        ),
        in_specs=[smem] + [vmem] * 5,
        out_specs=(vmem,) * 6,
        scratch_shapes=[pltpu.VMEM((count, PAD, PAD, cf), F32)],
        compiler_params=limit(28),
        name="fine_forward",
    )(last, features, features_below, g1, fine_project_in, fine_project_out)
    mid_below = shift(mid_head, -1)

    spot, rows = {}, 0
    for name, size in (
        ("coarse_in", 3 * cc),
        ("coarse_out", cc),
        ("merge", 4 * cf),
        ("expand", units // cc * cf),
        ("contract", units // cc * cf),
        ("gains", 8),
        ("fine", 2 * cf + 8),
    ):
        spot[name] = rows
        rows += size
    grain = 8 * STREAMS * devices
    total_rows = -(-rows // grain) * grain
    out_slab, out_tail, dmid, dmid_tail, packed = pl.pallas_call(
        functools.partial(middle, grad_scale, spot),
        out_shape=(
            shape(low, narrow, cc),
            shape(SHIFT, narrow, cc),
            shape(height, breadth, cf),
            shape(SHIFT, breadth, cf),
            shape(total_rows, cc),
        ),
        in_specs=[smem] + [vmem] * 12,
        out_specs=(vmem,) * 5,
        scratch_shapes=[pltpu.VMEM((4 * TOK, units), F32)] * 2
        + [pltpu.VMEM((4, PAD, PAD, cf), F32), pltpu.VMEM((1, PAD, PAD, cc), F32)],
        compiler_params=limit(40),
        name="middle",
    )(
        last,
        mid,
        mid_below,
        cotangent,
        cotangent_below,
        fine_gain_two.reshape(1, cf),
        fine_expand,
        fine_contract.T,
        merge_gain.reshape(4, cf),
        merge_weight,
        coarse_gain.reshape(1, cc),
        coarse_project_in,
        coarse_project_out,
    )
    dmid_above = shift(dmid_tail, 1)
    out_above = shift(out_tail, 1)
    dx, dx_tail, packed = pl.pallas_call(
        functools.partial(fine_backward, grad_scale, spot["fine"], win_cols),
        out_shape=(
            shape(height, breadth, cf),
            shape(SHIFT, breadth, cf),
            shape(*packed.shape),
        ),
        in_specs=[vmem] * 9 + [anywhere],
        out_specs=(vmem, vmem, anywhere),
        scratch_shapes=[
            pltpu.VMEM((2 * cf + 8, cc), F32),
            pltpu.VMEM((count, PAD, PAD, cf), F32),
            pltpu.SemaphoreType.DMA(()),
        ],
        input_output_aliases={9: 2},
        compiler_params=limit(28),
        name="fine_backward",
    )(dmid, dmid_above, x1, g1, fine_project_in, fine_project_out, qkv, weights, ctx, packed)
    dx_above = shift(dx_tail, 1)
    summed = all_sum(packed, devices)
    final = pl.pallas_call(
        functools.partial(unpack, spot, cf, cc),
        out_shape=(
            shape(low, narrow, cc),
            shape(height, breadth, cf),
            shape(1, cf),
            shape(cf, 3 * cf),
            shape(cf, cf),
            shape(1, cf),
            shape(cf, units),
            shape(cf, units),
            shape(1, 4 * cf),
            shape(4 * cf, cc),
            shape(1, cc),
            shape(cc, 3 * cc),
            shape(cc, cc),
        ),
        in_specs=[vmem] * 5,
        out_specs=(anywhere, anywhere, vmem, vmem, vmem, vmem, anywhere, anywhere, vmem, anywhere, vmem, anywhere, anywhere),
        scratch_shapes=[pltpu.SemaphoreType.DMA((6 + 3 + 2 * (units // cc),))],
        compiler_params=limit(20),
        name="unpack",
    )(summed, out_slab, out_above, dx, dx_above)
    final = list(final)
    final[7] = final[7].T
    for i in (2, 5, 8, 10):
        final[i] = final[i].reshape(-1)
    return tuple(final)


def solution(mesh):
    tokens = P(("groups", "rows"), None, None)
    vector, matrix = P("groups"), P("groups", None)
    in_specs = (tokens,) + (P(),) * 11 + (tokens,)
    out_specs = (
        tokens,
        tokens,
        vector,
        matrix,
        matrix,
        vector,
        matrix,
        matrix,
        vector,
        matrix,
        vector,
        matrix,
        matrix,
    )
    return jax.shard_map(shards, mesh=mesh, in_specs=in_specs, out_specs=out_specs, check_vma=False)
```
